256 devices in a mesh: section: 8 (over y_hi, x), ctx: 32 (over y_lo, z, core).
Axes of the slice: x: 4, y: 4 (y_hi: 2, y_lo: 2; y = y_hi * 2 + y_lo), z: 8, core: 2. Of those that a mesh axis runs over, the one named last changes fastest.
Arguments:
- projected: bfloat16 [8, 12288, 3072], P('section', 'ctx'), may hold values from -64 to 64
- grad_out: bfloat16 [8, 12288, 3072], P('section', 'ctx'), may hold values from -6 to 6
- doc_lengths: int32 [31], replicated, may hold values from 1 to 768, as said below
Outputs:
- grad_kv: float32 [12288, 2048], P('ctx')
The draws below stay inside these ranges and needn't reach their ends.
Inputs may be any that keep to these rules, and one draw needn't show every extreme that they name: `doc_lengths`: the lengths sum to 12288; the first document is shorter than 384 tokens and the second has exactly 768.
All inputs are finite; a program needn't handle non-finite values.
Results may differ from the reference program's by a relative error of at most 0.0031.
Values may be sent and summed in bfloat16 or wider, within the bound.
No kernel may reach another device: no remote copies, remote signals or barrier semaphores. Data moves between devices by JAX's collectives and lax.ppermute only.
A program may use at most 128 MiB of HBM per device.

```python
import math
import jax
import jax.numpy as jnp
from jax import lax

HEAD_SIZE = 128
KV_HEAD_COUNT = 8
QUERY_PER_KV = 3
QUERY_HEADS = 24
BLOCK_TOKENS = 384
SECTIONS = 8
WINDOW_TOKENS = 12288
DOC_MAX = 768
DOCS = 31


def draw_projected(key, part):
    block_offset = jnp.clip(jax.random.normal(key, (SECTIONS, WINDOW_TOKENS, QUERY_HEADS * HEAD_SIZE), jnp.float32), -6.0, 6.0)
    return block_offset.astype(jnp.bfloat16)


def draw_doc_lengths(key, part):
    key_first, key_pairs = jax.random.split(jax.random.fold_in(key, 23))
    first_len = jax.random.randint(key_first, (1,), 1, BLOCK_TOKENS, jnp.int32)
    pair_count = (DOCS - 3) // 2
    offsets = jax.random.randint(key_pairs, (pair_count,), -(BLOCK_TOKENS - 1), BLOCK_TOKENS, jnp.int32)
    paired = jnp.stack([BLOCK_TOKENS + offsets, BLOCK_TOKENS - offsets], axis=1).reshape(-1)
    longest = jnp.full((1,), DOC_MAX, jnp.int32)
    closing = 2 * BLOCK_TOKENS - first_len
    return jnp.concatenate([first_len, longest, paired.astype(jnp.int32), closing]).astype(jnp.int32)


def shard_levels(rng, extent, shards, smallest, high):
    factor_of = 1.0
    for dim, shards_of in shards:
        heights = jax.random.uniform(jax.random.fold_in(jax.random.fold_in(rng, 6), dim), (shards_of,), jnp.float32, smallest / len(shards), high / len(shards))
        factor_of = factor_of * jnp.repeat(jnp.exp(heights), extent[dim] // shards_of).reshape((-1,) + (1,) * (len(extent) - 1 - dim))
    return factor_of


def gaussian(rng, shape, deviation, limit, pieces=(), kind=jnp.bfloat16):
    gain = shard_levels(rng, shape, pieces, -0.22, 0.18) if pieces else 1.0
    result = jax.random.normal(rng, shape, jnp.float32) * deviation * gain
    return jnp.minimum(jnp.maximum(result, -limit), limit).astype(kind)


def setup_inputs(seed: int = 0) -> dict:
    key_of = jax.random.split(jax.random.key(seed), 4)
    return {
        "projected": draw_projected(jax.random.fold_in(key_of[3], 71), 0),
        "grad_out": gaussian(key_of[1], (SECTIONS, WINDOW_TOKENS, QUERY_HEADS * HEAD_SIZE), 1.0, 6.0, ((0, 8), (1, 32))),
        "doc_lengths": draw_doc_lengths(jax.random.fold_in(key_of[3], 71), 0),
    }


MASKED_SCORE = -1e+30

def document_of(places, doc_ends):
    return lax.optimization_barrier(jnp.sum((doc_ends[None, :] <= places[:, None]).astype(jnp.int32), axis=1)).astype(jnp.int32)

def reference(projected, grad_out, doc_lengths):
    section_count = projected.shape[0]
    shared_width = KV_HEAD_COUNT * HEAD_SIZE
    out_width = 2 * shared_width
    span_row_count = DOC_MAX + BLOCK_TOKENS
    score_scale = 1.0 / math.sqrt(HEAD_SIZE)
    highest = lax.Precision.HIGHEST
    doc_ends = jnp.cumsum(doc_lengths).astype(jnp.int32)
    padded = jnp.concatenate([jnp.zeros((DOC_MAX, out_width), projected.dtype), projected[0][:, :out_width]], axis=0).astype(jnp.float32)
    key_full = padded[:, :shared_width]
    value_full = padded[:, shared_width:]
    summed = jnp.zeros((DOC_MAX + WINDOW_TOKENS, out_width), jnp.float32)
    for section_index in range(1, section_count):
        query_full = projected[section_index].astype(jnp.float32)
        gradient_full = grad_out[section_index].astype(jnp.float32)

        def step_block(block_index, accum):
            first_row = (block_index * BLOCK_TOKENS).astype(jnp.int32)
            query_slice = lax.dynamic_slice_in_dim(query_full, first_row, BLOCK_TOKENS, 0).reshape(BLOCK_TOKENS, KV_HEAD_COUNT, QUERY_PER_KV, HEAD_SIZE)
            gradient_rows = lax.dynamic_slice_in_dim(gradient_full, first_row, BLOCK_TOKENS, 0).reshape(BLOCK_TOKENS, KV_HEAD_COUNT, QUERY_PER_KV, HEAD_SIZE)
            key_slice = lax.dynamic_slice_in_dim(key_full, first_row, span_row_count, 0).reshape(span_row_count, KV_HEAD_COUNT, HEAD_SIZE)
            value_slice = lax.dynamic_slice_in_dim(value_full, first_row, span_row_count, 0).reshape(span_row_count, KV_HEAD_COUNT, HEAD_SIZE)
            query_place = first_row + jnp.arange(BLOCK_TOKENS, dtype=jnp.int32)
            key_place = first_row - DOC_MAX + jnp.arange(span_row_count, dtype=jnp.int32)
            same_doc = document_of(query_place, doc_ends)[:, None] == document_of(key_place, doc_ends)[None, :]
            allowed = same_doc & (key_place[None, :] <= query_place[:, None]) & (key_place[None, :] >= 0)
            scores = jnp.einsum('qgah,kgh->gaqk', query_slice, key_slice, precision=highest) * score_scale
            scores = jnp.where(allowed[None, None], scores, MASKED_SCORE)
            row_top = lax.optimization_barrier(jnp.max(scores, axis=3, keepdims=True))
            powers = jnp.exp(scores - row_top)
            attn_weight = powers / lax.optimization_barrier(jnp.sum(powers, axis=3, keepdims=True))
            attn_half = lax.optimization_barrier(attn_weight.astype(jnp.bfloat16)).astype(jnp.float32)
            attended = jnp.einsum('gaqk,kgh->qgah', attn_half, value_slice, precision=highest)
            delta_rows = jnp.transpose(lax.optimization_barrier(jnp.sum(gradient_rows * attended, axis=3)), (1, 2, 0))
            grad_prob = jnp.einsum('qgah,kgh->gaqk', gradient_rows, value_slice, precision=highest)
            grad_score = attn_weight * (grad_prob - delta_rows[..., None])
            grad_score = lax.optimization_barrier(grad_score.astype(jnp.bfloat16)).astype(jnp.float32)
            grad_key = jnp.einsum('gaqk,qgah->kgh', grad_score, query_slice, precision=highest) * score_scale
            grad_value = jnp.einsum('gaqk,qgah->kgh', attn_half, gradient_rows, precision=highest)
            update = jnp.concatenate([grad_key.reshape(span_row_count, shared_width), grad_value.reshape(span_row_count, shared_width)], axis=1)
            current = lax.dynamic_slice_in_dim(accum, first_row, span_row_count, 0)
            return lax.dynamic_update_slice_in_dim(accum, current + update, first_row, 0)
        summed = lax.fori_loop(0, WINDOW_TOKENS // BLOCK_TOKENS, step_block, summed)
    return summed[DOC_MAX:]
```

```python
import functools
import math

import jax
import jax.numpy as jnp
from jax import lax
from jax.experimental import pallas as pl
from jax.experimental.pallas import tpu as pltpu
from jax.sharding import PartitionSpec as P

HEAD = 128
HEADS = 8
GROUP = 3
WIDTH = GROUP * HEAD
TOK = 384
TILE = 128
REACH = 2
ROWS = (REACH + 1) * TOK
SECTIONS = 8
XS = 4
DOCS = 31
SPAN = 7
NEG = -1e30
SCALE = 1.0 / math.sqrt(HEAD)
EXP2_SCALE = SCALE * math.log2(math.e)


def shifted_section(section, offset):
    row = lax.rem(section // XS + offset // XS, 2)
    col = lax.rem(lax.rem(section, XS) + offset % XS, XS)
    return row * XS + col


def offset_pairs(offset, skip_first):
    pairs = []
    for source in range(SECTIONS):
        if skip_first and source == 0:
            continue
        row = (source // XS + offset // XS) % 2
        col = (source % XS + offset % XS) % XS
        pairs.append((source, row * XS + col))
    return pairs


def pack_kernel(section_ref, proj_ref, grad_ref, *refs):
    chunks = refs[:SECTIONS]
    shared = refs[SECTIONS : 2 * SECTIONS]
    buf, kv_buf, in_sem, out_sem, kv_in_sem, kv_out_sem = refs[2 * SECTIONS :]
    section = section_ref[0]

    def chunk_in(offset):
        columns = pl.ds(pl.multiple_of(shifted_section(section, offset) * WIDTH, HEAD), WIDTH)
        return [
            pltpu.make_async_copy(src.at[:, columns], buf.at[offset, part], in_sem.at[offset, part])
            for part, src in enumerate((proj_ref, grad_ref))
        ]

    def chunk_out(offset):
        return pltpu.make_async_copy(buf.at[offset], chunks[offset], out_sem.at[offset])

    def shared_in(head):
        return [
            pltpu.make_async_copy(
                proj_ref.at[:, pl.ds((part * HEADS + head) * HEAD, HEAD)],
                kv_buf.at[head, :, pl.ds(part * HEAD, HEAD)],
                kv_in_sem.at[head, part],
            )
            for part in range(2)
        ]

    def shared_out(head):
        return pltpu.make_async_copy(kv_buf.at[head], shared[head], kv_out_sem.at[head])

    @pl.when(section == 0)
    def _():
        for head in range(HEADS):
            for copy in shared_in(head):
                copy.start()

    for offset in range(SECTIONS):
        for copy in chunk_in(offset):
            copy.start()

    @pl.when(section == 0)
    def _():
        for head in range(HEADS):
            for copy in shared_in(head):
                copy.wait()
            shared_out(head).start()

    for offset in range(SECTIONS):
        for copy in chunk_in(offset):
            copy.wait()
        chunk_out(offset).start()
    for offset in range(SECTIONS):
        chunk_out(offset).wait()

    @pl.when(section == 0)
    def _():
        for head in range(HEADS):
            shared_out(head).wait()


def pack(section, proj, grad):
    chunk = jax.ShapeDtypeStruct((2, TOK, WIDTH), jnp.bfloat16)
    shared = jax.ShapeDtypeStruct((TOK, 2 * HEAD), jnp.bfloat16)
    hbm = pl.BlockSpec(memory_space=pl.ANY)
    outs = pl.pallas_call(
        pack_kernel,
        out_shape=[chunk] * SECTIONS + [shared] * SECTIONS,
        in_specs=[pl.BlockSpec(memory_space=pltpu.SMEM), hbm, hbm],
        out_specs=[hbm] * (2 * SECTIONS),
        scratch_shapes=[
            pltpu.VMEM((SECTIONS, 2, TOK, WIDTH), jnp.bfloat16),
            pltpu.VMEM((HEADS, TOK, 2 * HEAD), jnp.bfloat16),
            pltpu.SemaphoreType.DMA((SECTIONS, 2)),
            pltpu.SemaphoreType.DMA((SECTIONS,)),
            pltpu.SemaphoreType.DMA((HEADS, 2)),
            pltpu.SemaphoreType.DMA((HEADS,)),
        ],
        cost_estimate=pl.CostEstimate(flops=0, bytes_accessed=12_000_000, transcendentals=0),
        name="pack",
    )(section, proj, grad)
    return outs[:SECTIONS], outs[SECTIONS:]


def dot_nt(a, b):
    return lax.dot_general(a, b, (((1,), (1,)), ((), ())), preferred_element_type=jnp.float32)


def dot_nn(a, b):
    return lax.dot_general(a, b, (((1,), (0,)), ((), ())), preferred_element_type=jnp.float32)


def attend_kernel(count, first, last, skip_own, place_ref, docs_ref, *refs):
    chunks = refs[:count]
    refs = refs[count:]
    if first:
        window = refs[:3]
        refs = refs[3:]
    else:
        keys_in, total_in = refs[:2]
        refs = refs[2:]
    if last:
        outs = refs[:3]
        keys, total, bias, scores, probs = refs[3:]
    elif first:
        keys, total, bias, scores, probs = refs
    else:
        total, bias, scores, probs = refs
    if first:
        for piece in range(3):
            keys[piece * TOK : (piece + 1) * TOK, :] = window[piece][...]
        total[...] = jnp.zeros_like(total)
    else:
        total[...] = total_in[...]
        if last:
            keys = keys_in
        else:
            keys = keys_in
    ctx = place_ref[0]
    section = place_ref[1]
    base = (ctx - REACH) * TOK

    def query_tile(tile, carry):
        row = pl.multiple_of(tile * TILE, TILE)
        place = ctx * TOK + row
        places = place + lax.broadcasted_iota(jnp.int32, (8, TILE), 1)
        end = jnp.int32(0)
        begin = jnp.int32(0)
        begins = jnp.zeros((8, TILE), jnp.int32)
        for doc in range(DOCS):
            end = end + docs_ref[doc]
            begin = jnp.where(end <= place, end, begin)
            begins = jnp.where(end <= places, end, begins)
        low = (begins - base)[0:1]
        high = (places - base)[0:1]
        start = jnp.maximum(lax.shift_right_arithmetic(begin - base, 7), tile)
        steps = jnp.minimum(tile + SPAN - start, SPAN)

        def key_row(step):
            return pl.multiple_of((start + step) * TILE, TILE)

        def bias_step(step, carry):
            spot = key_row(step) + lax.broadcasted_iota(jnp.int32, (TILE, TILE), 0)
            inside = (spot >= low) & (spot <= high)
            bias[step] = jnp.where(inside, 0.0, NEG)
            return carry

        lax.fori_loop(0, steps, bias_step, 0)

        def stacked(chunk, part):
            rows = pl.ds(row, TILE)
            return jnp.concatenate(
                [chunk[part, rows, h * HEAD : (h + 1) * HEAD] for h in range(GROUP)], axis=0
            )

        def top_step(step, tops):
            key = keys[pl.ds(key_row(step), TILE), 0:HEAD]
            hide = jnp.concatenate([bias[step]] * GROUP, axis=1)
            result = []
            for index in range(count):
                score = dot_nt(key, stacked(chunks[index], 0)) + hide
                scores[index, step] = score
                folded = jnp.max(score.reshape(TILE // 8, 8, WIDTH), axis=0)
                result.append(jnp.maximum(tops[index], folded))
            return tuple(result)

        tops = lax.fori_loop(
            0, steps, top_step, tuple(jnp.full((8, WIDTH), NEG, jnp.float32) for _ in range(count))
        )
        tops = [jnp.max(top, axis=0, keepdims=True) * EXP2_SCALE for top in tops]

        def power_step(step, sums):
            value = keys[pl.ds(key_row(step), TILE), HEAD : 2 * HEAD]
            result = []
            for index in range(count):
                power = jnp.exp2(scores[index, step] * EXP2_SCALE - tops[index])
                slope = dot_nt(value, stacked(chunks[index], 1))
                probs[index, step] = power
                scores[index, step] = slope
                weight, delta = sums[index]
                weight = weight + jnp.sum(power.reshape(TILE // 8, 8, WIDTH), axis=0)
                delta = delta + jnp.sum((power * slope).reshape(TILE // 8, 8, WIDTH), axis=0)
                result.append((weight, delta))
            return tuple(result)

        zero = jnp.zeros((8, WIDTH), jnp.float32)
        sums = lax.fori_loop(0, steps, power_step, tuple((zero, zero) for _ in range(count)))
        scales = []
        deltas = []
        for weight, delta in sums:
            scale = 1.0 / jnp.sum(weight, axis=0, keepdims=True)
            scales.append(scale)
            deltas.append(jnp.sum(delta, axis=0, keepdims=True) * scale)

        def grad_step(step, carry):
            rows = pl.ds(key_row(step), TILE)
            grad_key = total[rows, 0:HEAD]
            grad_value = total[rows, HEAD : 2 * HEAD]
            for index in range(count):
                prob = probs[index, step] * scales[index]
                slope = (prob * (scores[index, step] - deltas[index])).astype(jnp.bfloat16)
                grad_value += dot_nn(prob.astype(jnp.bfloat16), stacked(chunks[index], 1))
                grad_key += dot_nn(slope, stacked(chunks[index], 0))
            total[rows, 0:HEAD] = grad_key
            total[rows, HEAD : 2 * HEAD] = grad_value
            return carry

        lax.fori_loop(0, steps, grad_step, 0)
        return carry

    tiles = TOK // TILE
    if skip_own:
        tiles = jnp.where(section == 0, 0, tiles)
    lax.fori_loop(0, tiles, query_tile, 0)
    if last:
        factor = lax.broadcasted_iota(jnp.int32, (1, 2 * HEAD), 1) < HEAD
        factor = jnp.where(factor, SCALE, 1.0)
        for piece in range(3):
            block = total[piece * TOK : (piece + 1) * TOK, :] * factor
            outs[piece][...] = block.astype(outs[piece].dtype)


def attend(place, docs, chunks, window=None, keys=None, total=None, last=False, skip_own=False):
    count = len(chunks)
    first = window is not None
    smem = pl.BlockSpec(memory_space=pltpu.SMEM)
    vmem = pl.BlockSpec(memory_space=pltpu.VMEM)
    scratch = [
        pltpu.VMEM((SPAN, TILE, TILE), jnp.float32),
        pltpu.VMEM((count, SPAN, TILE, WIDTH), jnp.float32),
        pltpu.VMEM((count, SPAN, TILE, WIDTH), jnp.float32),
    ]
    keys_shape = ((ROWS, 2 * HEAD), jnp.bfloat16)
    total_shape = ((ROWS, 2 * HEAD), jnp.float32)
    operands = list(chunks)
    if first:
        operands += list(window)
        out_shape = [jax.ShapeDtypeStruct(*keys_shape), jax.ShapeDtypeStruct(*total_shape)]
    else:
        operands += [keys, total]
        out_shape = [jax.ShapeDtypeStruct(*total_shape)]
    if last:
        out_shape = [
            jax.ShapeDtypeStruct((TOK, 2 * HEAD), kind)
            for kind in (jnp.float32, jnp.float32, jnp.float32)
        ]
        scratch = [pltpu.VMEM(*keys_shape), pltpu.VMEM(*total_shape)] + scratch
    return pl.pallas_call(
        functools.partial(attend_kernel, count, first, last, skip_own),
        out_shape=out_shape,
        in_specs=[smem, smem] + [vmem] * len(operands),
        out_specs=[vmem] * len(out_shape),
        scratch_shapes=scratch,
        cost_estimate=pl.CostEstimate(
            flops=count * 2_500_000_000, bytes_accessed=count * 600_000, transcendentals=0
        ),
        name=f"attend_{count}",
    )(place, docs, *operands)


def assemble_kernel(section_ref, *refs):
    pieces = refs[:SECTIONS]
    out = refs[SECTIONS]
    section = section_ref[0]
    for offset in range(SECTIONS):
        row = lax.rem(section // XS + 2 - offset // XS, 2)
        col = lax.rem(lax.rem(section, XS) + XS - offset % XS, XS)
        head = row * XS + col
        for part in range(2):
            columns = pl.ds(pl.multiple_of((part * HEADS + head) * HEAD, HEAD), HEAD)
            piece = pieces[offset][:, part * HEAD : (part + 1) * HEAD]
            out[:, columns] = piece.astype(jnp.float32)


def assemble(section, pieces):
    return pl.pallas_call(
        assemble_kernel,
        out_shape=jax.ShapeDtypeStruct((TOK, 2 * HEADS * HEAD), jnp.float32),
        grid=(3,),
        in_specs=[pl.BlockSpec(memory_space=pltpu.SMEM)]
        + [pl.BlockSpec((TOK // 3, 2 * HEAD), lambda i: (i, 0))] * SECTIONS,
        out_specs=pl.BlockSpec((TOK // 3, 2 * HEADS * HEAD), lambda i: (i, 0)),
        cost_estimate=pl.CostEstimate(flops=0, bytes_accessed=5_000_000, transcendentals=0),
        name="assemble",
    )(section, *pieces)


def on_device(projected, grad_out, doc_lengths):
    section = lax.axis_index("section").astype(jnp.int32)
    ctx = lax.axis_index("ctx").astype(jnp.int32)
    section_arr = section.reshape(1)
    place = jnp.stack([ctx, section])
    count = lax.axis_size("ctx")
    sent, shared = pack(section_arr, projected[0], grad_out[0])

    def moved(offset):
        return lax.ppermute(sent[offset], "section", offset_pairs(offset, True))

    chunk = {0: sent[0]}
    for offset in (1, 3, 4):
        chunk[offset] = moved(offset)
    own = jnp.where(section == 0, shared[0], 0)
    for head in range(1, HEADS):
        own = own + lax.ppermute(shared[head], "section", [(0, head)])
    for offset in (2, 5, 7, 6):
        chunk[offset] = moved(offset)
    window = [
        lax.ppermute(own, "ctx", [(i, i + step) for i in range(count - step)]) for step in (2, 1)
    ]
    keys, total = attend(place, doc_lengths, [chunk[0]], window=window + [own], skip_own=True)
    (total,) = attend(place, doc_lengths, [chunk[o] for o in (1, 3, 4)], keys=keys, total=total)
    (total,) = attend(place, doc_lengths, [chunk[o] for o in (2, 5)], keys=keys, total=total)
    (total,) = attend(place, doc_lengths, [chunk[o] for o in (7,)], keys=keys, total=total)
    far, near, here = attend(
        place, doc_lengths, [chunk[o] for o in (6,)], keys=keys, total=total, last=True
    )
    far = lax.ppermute(far, "ctx", [(i, i - 2) for i in range(2, count)])
    near = lax.ppermute(near, "ctx", [(i, i - 1) for i in range(1, count)])
    final = (here + near + far).astype(jnp.bfloat16)
    pieces = [final]
    for offset in range(1, SECTIONS):
        pieces.append(lax.ppermute(final, "section", offset_pairs(offset, False)))
    return assemble(section_arr, pieces)


def solution(mesh):
    return jax.shard_map(
        on_device,
        mesh=mesh,
        in_specs=(P("section", "ctx", None), P("section", "ctx", None), P()),
        out_specs=P("ctx", None),
        check_vma=False,
    )
```

```python
import functools
import math

import jax
import jax.numpy as jnp
from jax import lax
from jax.experimental import pallas as pl
from jax.experimental.pallas import tpu as pltpu
from jax.sharding import PartitionSpec as P

HEAD = 128
HEADS = 8
GROUP = 3
TOK = 384
WIDTH = GROUP * HEAD
TILE = 128
STEP = 256
REACH = 2
ROWS = (REACH + 1) * TOK
PADDED = ROWS + TILE
SECTIONS = 8
XS = 4
DOCS = 31
SPAN = 7
STEPS = 4
SENDS = (6, 5, 7, 4, 2, 1, 3)
ORDER = (*SENDS, 0)
WAVES = ((0, 6, 5), (7, 4, 2, 1, 3))
VMEM_LIMIT = 40 * 1024 * 1024
NEG = -1e30
SCALE = 1.0 / math.sqrt(HEAD)
EXP2_SCALE = SCALE * math.log2(math.e)


def pack_kernel(section_ref, proj_ref, grad_ref, *refs):
    chunks = refs[:SECTIONS]
    shared = refs[SECTIONS : 2 * SECTIONS]
    buf, kv_buf, in_sem, out_sem, kv_in_sem, kv_out_sem = refs[2 * SECTIONS :]
    section = section_ref[0]

    def chunk_in(offset, side):
        row = lax.rem(section // XS + offset // XS, 2)
        col = lax.rem(lax.rem(section, XS) + offset % XS, XS)
        dest = row * XS + col
        return pltpu.make_async_copy(
            (proj_ref, grad_ref)[side].at[:, pl.ds(pl.multiple_of(dest * WIDTH, HEAD), WIDTH)],
            buf.at[offset, :, pl.ds(side * WIDTH, WIDTH)],
            in_sem.at[offset, side],
        )

    def chunk_out(offset):
        return pltpu.make_async_copy(buf.at[offset], chunks[offset], out_sem.at[offset])

    def shared_in(head, side):
        return pltpu.make_async_copy(
            proj_ref.at[:, pl.ds((side * HEADS + head) * HEAD, HEAD)],
            kv_buf.at[head, :, pl.ds(side * HEAD, HEAD)],
            kv_in_sem.at[head, side],
        )

    def shared_out(head):
        return pltpu.make_async_copy(kv_buf.at[head], shared[head], kv_out_sem.at[head])

    @pl.when(section == 0)
    def _():
        buf[0] = jnp.zeros((TOK, 2 * WIDTH), jnp.bfloat16)
        chunk_out(0).start()
        for head in range(HEADS):
            for side in range(2):
                shared_in(head, side).start()
        for head in range(HEADS):
            for side in range(2):
                shared_in(head, side).wait()
            shared_out(head).start()
        for head in range(HEADS):
            shared_out(head).wait()
        chunk_out(0).wait()

    @pl.when(section != 0)
    def _():
        for offset in ORDER:
            for side in range(2):
                chunk_in(offset, side).start()
        for offset in ORDER:
            for side in range(2):
                chunk_in(offset, side).wait()
            chunk_out(offset).start()
        for offset in ORDER:
            chunk_out(offset).wait()


def pack(section, proj, grad):
    chunk = jax.ShapeDtypeStruct((TOK, 2 * WIDTH), jnp.bfloat16)
    shared = jax.ShapeDtypeStruct((TOK, 2 * HEAD), jnp.bfloat16)
    hbm = pl.BlockSpec(memory_space=pl.ANY)
    outs = pl.pallas_call(
        pack_kernel,
        out_shape=[chunk] * SECTIONS + [shared] * SECTIONS,
        in_specs=[pl.BlockSpec(memory_space=pltpu.SMEM), hbm, hbm],
        out_specs=[hbm] * (2 * SECTIONS),
        scratch_shapes=[
            pltpu.VMEM((SECTIONS, *chunk.shape), jnp.bfloat16),
            pltpu.VMEM((HEADS, *shared.shape), jnp.bfloat16),
            pltpu.SemaphoreType.DMA((SECTIONS, 2)),
            pltpu.SemaphoreType.DMA((SECTIONS,)),
            pltpu.SemaphoreType.DMA((HEADS, 2)),
            pltpu.SemaphoreType.DMA((HEADS,)),
        ],
        cost_estimate=pl.CostEstimate(flops=0, bytes_accessed=9_600_000, transcendentals=0),
        name="pack",
    )(section, proj, grad)
    return outs[:SECTIONS], outs[SECTIONS:]


def dot_nt(a, b):
    return lax.dot_general(a, b, (((1,), (1,)), ((), ())), preferred_element_type=jnp.float32)


def dot_nn(a, b):
    return lax.dot_general(a, b, (((1,), (0,)), ((), ())), preferred_element_type=jnp.float32)


def fold(reduce, block):
    return reduce(block.reshape(block.shape[0] // 8, 8, block.shape[1]), axis=0)


def attend_kernel(first, last, count, place_ref, docs_ref, *refs):
    chunks, refs = refs[:count], refs[count:]
    if first:
        window, (keys, total), refs = refs[:3], refs[3:5], refs[5:]
        for piece in range(3):
            keys[piece * TOK : (piece + 1) * TOK, :] = window[piece][...]
        keys[ROWS:PADDED, :] = jnp.zeros((TILE, 2 * HEAD), jnp.bfloat16)
        total[...] = jnp.zeros_like(total)
    elif last:
        (keys, total_in), outs, total, refs = refs[:2], refs[2:5], refs[5], refs[6:]
        total[...] = total_in[...]
    else:
        (keys, total_in, total), refs = refs[:3], refs[3:]
        total[...] = total_in[...]
    scores, probs = refs
    base = (place_ref[0] - REACH) * TOK
    batches = range(count)

    def bounds(tile):
        row = pl.multiple_of(tile * TILE, TILE)
        place = base + ROWS - TOK + row
        places = place + lax.broadcasted_iota(jnp.int32, (8, TILE), 1)
        end = jnp.int32(0)
        begin = jnp.int32(0)
        begins = jnp.zeros((8, TILE), jnp.int32)
        for doc in range(DOCS):
            end = end + docs_ref[doc]
            begin = jnp.where(end <= place, end, begin)
            begins = jnp.where(end <= places, end, begins)
        low = (begins - base)[0:1]
        high = (places - base)[0:1]
        start = jnp.maximum(lax.shift_right_arithmetic(begin - base, 7), tile)
        steps = jnp.minimum(lax.shift_right_arithmetic(tile + SPAN - start + 1, 1), STEPS)
        return row, start, steps, low, high

    def grads(steps, row, start, low, high):
        rows = pl.ds(row, TILE)

        def repeat(body, carry):
            for step in range(steps):
                carry = body(step, carry)
            return carry

        def key_rows(step):
            return pl.multiple_of(start * TILE + step * STEP, TILE)

        def joined(batch, side):
            return jnp.concatenate(
                [
                    chunks[batch][rows, (side * GROUP + h) * HEAD : (side * GROUP + h + 1) * HEAD]
                    for h in range(GROUP)
                ],
                axis=0,
            )

        def lanes(batch):
            return slice(batch * WIDTH, (batch + 1) * WIDTH)

        def top_step(step, tops):
            first_key = key_rows(step)
            key = keys[pl.ds(first_key, STEP), 0:HEAD]
            spot = first_key + lax.broadcasted_iota(jnp.int32, (STEP, TILE), 0)
            bias = jnp.where((spot >= low) & (spot <= high), 0.0, NEG)
            result = []
            for batch in batches:
                hide = jnp.concatenate([bias] * GROUP, axis=1)
                score = dot_nt(key, joined(batch, 0)) + hide
                scores[step, :, lanes(batch)] = score
                result.append(jnp.maximum(tops[batch], fold(jnp.max, score)))
            return tuple(result)

        def empty(value):
            return tuple(jnp.full((8, WIDTH), value, jnp.float32) for _ in batches)

        tops = repeat(top_step, empty(NEG))
        tops = [jnp.max(top, axis=0, keepdims=True) * EXP2_SCALE for top in tops]

        def power_step(step, sums):
            value = keys[pl.ds(key_rows(step), STEP), HEAD : 2 * HEAD]
            result = []
            for batch in batches:
                power = jnp.exp2(scores[step, :, lanes(batch)] * EXP2_SCALE - tops[batch])
                slope = dot_nt(value, joined(batch, 1))
                probs[step, :, lanes(batch)] = power
                scores[step, :, lanes(batch)] = slope
                weight, delta = sums[0][batch], sums[1][batch]
                result.append(
                    (weight + fold(jnp.sum, power), delta + fold(jnp.sum, power * slope))
                )
            return tuple(zip(*result))

        sums = repeat(power_step, (empty(0.0), empty(0.0)))
        scales = [1.0 / jnp.sum(weight, axis=0, keepdims=True) for weight in sums[0]]
        deltas = [
            jnp.sum(delta, axis=0, keepdims=True) * scale for delta, scale in zip(sums[1], scales)
        ]

        def grad_step(step, carry):
            spots = pl.ds(key_rows(step), STEP)
            grad_key = total[spots, 0:HEAD]
            grad_value = total[spots, HEAD : 2 * HEAD]
            for batch in batches:
                prob = probs[step, :, lanes(batch)] * scales[batch]
                slope = prob * (scores[step, :, lanes(batch)] - deltas[batch])
                grad_value += dot_nn(prob.astype(jnp.bfloat16), joined(batch, 1))
                grad_key += dot_nn(slope.astype(jnp.bfloat16), joined(batch, 0))
            total[spots, 0:HEAD] = grad_key
            total[spots, HEAD : 2 * HEAD] = grad_value
            return carry

        repeat(grad_step, 0)

    def query_tile(tile, carry):
        row, start, steps, low, high = bounds(tile)
        for static in range(1, STEPS + 1):
            pl.when(steps == static)(
                functools.partial(grads, static, row, start, low, high)
            )
        return carry

    lax.fori_loop(0, TOK // TILE, query_tile, 0)
    if last:
        is_key = lax.broadcasted_iota(jnp.int32, (1, 2 * HEAD), 1) < HEAD
        factor = jnp.where(is_key, SCALE, 1.0)
        for piece in range(3):
            block = total[piece * TOK : (piece + 1) * TOK, :] * factor
            outs[piece][...] = block.astype(outs[piece].dtype)


def attend(place, docs, chunks, window=None, keys=None, total=None, last=False):
    first = window is not None
    count = len(chunks)
    smem = pl.BlockSpec(memory_space=pltpu.SMEM)
    vmem = pl.BlockSpec(memory_space=pltpu.VMEM)
    total_shape = ((PADDED, 2 * HEAD), jnp.float32)
    scratch = [pltpu.VMEM((STEPS, STEP, count * WIDTH), jnp.float32)] * 2
    out_shape = [jax.ShapeDtypeStruct(*total_shape)]
    if first:
        operands = [*chunks, *window]
        out_shape = [jax.ShapeDtypeStruct((PADDED, 2 * HEAD), jnp.bfloat16), *out_shape]
    else:
        operands = [*chunks, keys, total]
    if last:
        kinds = (jnp.bfloat16, jnp.bfloat16, jnp.float32)
        out_shape = [jax.ShapeDtypeStruct((TOK, 2 * HEAD), kind) for kind in kinds]
        scratch = [pltpu.VMEM(*total_shape), *scratch]
    return pl.pallas_call(
        functools.partial(attend_kernel, first, last, count),
        out_shape=out_shape,
        in_specs=[smem, smem] + [vmem] * len(operands),
        out_specs=[vmem] * len(out_shape),
        scratch_shapes=scratch,
        cost_estimate=pl.CostEstimate(
            flops=count * 3_000_000_000, bytes_accessed=count * 2_000_000, transcendentals=0
        ),
        compiler_params=pltpu.CompilerParams(vmem_limit_bytes=VMEM_LIMIT),
    )(place, docs, *operands)


def assemble_kernel(section_ref, *refs):
    pieces, out = refs[:SECTIONS], refs[SECTIONS]
    wide, out_sem = refs[SECTIONS + 1 :]
    section = section_ref[0]

    def write(offset, part):
        row = lax.rem(section // XS + 2 - offset // XS, 2)
        col = lax.rem(lax.rem(section, XS) + XS - offset % XS, XS)
        head = row * XS + col
        columns = pl.ds(pl.multiple_of((part * HEADS + head) * HEAD, HEAD), HEAD)
        return pltpu.make_async_copy(
            wide.at[offset, :, pl.ds(part * HEAD, HEAD)], out.at[:, columns], out_sem.at[offset, part]
        )

    for offset in range(SECTIONS):
        wide[offset] = pieces[offset][...].astype(jnp.float32)
        for part in range(2):
            write(offset, part).start()
    for offset in range(SECTIONS):
        for part in range(2):
            write(offset, part).wait()


def assemble(section, pieces):
    hbm = pl.BlockSpec(memory_space=pl.ANY)
    shape = (SECTIONS, TOK, 2 * HEAD)
    return pl.pallas_call(
        assemble_kernel,
        out_shape=jax.ShapeDtypeStruct((TOK, 2 * HEADS * HEAD), jnp.float32),
        in_specs=[pl.BlockSpec(memory_space=pltpu.SMEM)]
        + [pl.BlockSpec(memory_space=pltpu.VMEM)] * SECTIONS,
        out_specs=hbm,
        scratch_shapes=[
            pltpu.VMEM(shape, jnp.float32),
            pltpu.SemaphoreType.DMA((SECTIONS, 2)),
        ],
        cost_estimate=pl.CostEstimate(flops=0, bytes_accessed=5_000_000, transcendentals=0),
        compiler_params=pltpu.CompilerParams(vmem_limit_bytes=VMEM_LIMIT),
        name="assemble",
    )(section, *pieces)


def section_pairs(offset, skip=()):
    return [
        (s, (s // XS + offset // XS) % 2 * XS + (s % XS + offset % XS) % XS)
        for s in range(SECTIONS)
        if s not in skip
    ]


def sent(block, offset, skip=()):
    return lax.ppermute(block, "section", section_pairs(offset, skip))


def on_device(projected, grad_out, doc_lengths):
    section = lax.axis_index("section").astype(jnp.int32).reshape(1)
    place = lax.axis_index("ctx").astype(jnp.int32).reshape(1)
    count = lax.axis_size("ctx")
    chunks, shared = pack(section, projected[0], grad_out[0])
    chunk = {0: chunks[0]}
    for offset in SENDS:
        chunk[offset] = sent(chunks[offset], offset, (0,))
    own = jnp.where(section == 0, shared[0], 0)
    for head in range(1, HEADS):
        own = own + lax.ppermute(shared[head], "section", [(0, head)])
    window = [
        lax.ppermute(own, "ctx", [(i, i + step) for i in range(count - step)])
        for step in (2, 1)
    ]
    keys, total = attend(place, doc_lengths, [chunk[o] for o in WAVES[0]], window=window + [own])
    for wave in WAVES[1:-1]:
        (total,) = attend(
            place, doc_lengths, [chunk[o] for o in wave], keys=keys, total=total
        )
    far, near, here = attend(
        place, doc_lengths, [chunk[o] for o in WAVES[-1]], keys=keys, total=total, last=True
    )
    far = lax.ppermute(far, "ctx", [(i, i - 2) for i in range(2, count)])
    near = lax.ppermute(near, "ctx", [(i, i - 1) for i in range(1, count)])
    final = (here + near.astype(jnp.float32) + far.astype(jnp.float32)).astype(jnp.bfloat16)
    pieces = {0: final}
    for offset in (1, 3, 2):
        pieces[offset] = sent(final, offset)
    other = pieces[XS] = sent(final, XS)
    for offset in (1, 3, 2):
        pieces[XS + offset] = sent(other, offset)
    return assemble(section, [pieces[offset] for offset in range(SECTIONS)])


def solution(mesh):
    return jax.shard_map(
        on_device,
        mesh=mesh,
        in_specs=(P("section", "ctx", None), P("section", "ctx", None), P()),
        out_specs=P("ctx", None),
        check_vma=False,
    )
```
